32 devices in a mesh: seq: 8 (over z, x), exp: 4 (over y, core).
Axes of the slice: x: 2, y: 2, z: 4, core: 2. Of those that a mesh axis runs over, the one named last changes fastest.
Arguments:
- queries: bfloat16 [1024, 4096], P('seq', 'exp'), may hold values from -2 to 2
- keys: bfloat16 [1024, 4096], P('seq', 'exp'), may hold values from -2 to 2
- values: bfloat16 [1024, 4096], P('seq', 'exp'), may hold values from -6 to 6
- log_decay: float32 [1024, 32], P('seq', 'exp'), may hold values from -1 to 0, as said below
- residual: bfloat16 [1024, 4096], P(('seq', 'exp')), may hold values from -6 to 6
- attn_gain: float32 [4096], replicated, may hold values from 0.25 to 1.75
- moe_gain: float32 [4096], replicated, may hold values from 0.25 to 1.75
- expert_ids: int32 [1024, 2], P(('seq', 'exp')), may hold values from 0 to 3, all different within a row; in each aligned block of 32 rows (0 to 31, 32 to 63, ...) at most 24 rows name the same one
- gate_weights: float32 [1024, 2], P(('seq', 'exp')), may hold values from 0.2 to 1
- w_gate: bfloat16 [4, 9216, 4096], P('exp', 'seq'), may hold values from -0.09375 to 0.09375
- w_up: bfloat16 [4, 9216, 4096], P('exp', 'seq'), may hold values from -0.09375 to 0.09375
- w_down: bfloat16 [4, 9216, 4096], P('exp', 'seq'), may hold values from -0.0625 to 0.0625
Outputs:
- layer_out: bfloat16 [1024, 4096], P(('seq', 'exp'))
The draws below stay inside these ranges and needn't reach their ends.
Inputs may be any that keep to these rules, and one draw needn't show every extreme that they name: `expert_ids`: each token names two different experts. In each aligned block of 32 tokens (the tokens of one device) no expert is named by more than 24 tokens, a bound that some block reaches. `log_decay`: every entry is negative.
All inputs are finite; a program needn't handle non-finite values.
Results may differ from the reference program's by a relative error of at most 0.012.
Values may be sent and summed in bfloat16 or wider, within the bound.
A program may use at most 128 MiB of HBM per device.

```python
import math
import jax
import jax.numpy as jnp
import numpy as np
from jax import lax

HEAD_TOTAL = 32
HD = 128
FF = 9216
BLOCK = 128
D = 4096
EXPERTS = 4
TOK_DEV = 32
CAP = 24
TOKEN_TOTAL = 1024
N_SEQ = 8


def draw_log_decay(key, part):
    key_collection = jax.random.split(jax.random.fold_in(key, 17), 6)
    slow_share = 0.5
    slow_heads = jax.random.uniform(key_collection[0], (HEAD_TOTAL,)) < slow_share
    slow_rate = jnp.exp(jax.random.uniform(key_collection[1], (HEAD_TOTAL,), minval=math.log(0.2), maxval=math.log(1.0))) / TOKEN_TOTAL
    fast_rate = jnp.exp(jax.random.uniform(key_collection[2], (HEAD_TOTAL,), minval=math.log(1.0 / 50.0), maxval=math.log(1.0 / 30.0)))
    baseline_decay_rate = jnp.where(slow_heads, slow_rate, fast_rate)
    multiplier = jnp.exp(jax.random.uniform(key_collection[3], (TOKEN_TOTAL, HEAD_TOTAL), minval=math.log(0.5), maxval=math.log(2.0)))
    spike_rows = jax.random.uniform(key_collection[4], (TOKEN_TOTAL, 1)) < 2.0 / TOKEN_TOTAL
    spike_loss = jnp.log(jax.random.uniform(key_collection[5], (TOKEN_TOTAL, HEAD_TOTAL), minval=0.5, maxval=0.8))
    final_output = -(baseline_decay_rate[None, :] * multiplier) + jnp.where(spike_rows, spike_loss, 0.0)
    return final_output.astype(jnp.float32)


def steps_of(key, shape, pieces, smallest, largest):
    def one(axis_at, blocks):
        steps = jax.random.uniform(jax.random.fold_in(jax.random.fold_in(key, 6), axis_at), (blocks,), jnp.float32, smallest / len(pieces), largest / len(pieces))
        return jnp.repeat(jnp.exp(steps), shape[axis_at] // blocks).reshape((-1,) + (1,) * (len(shape) - axis_at - 1))

    level = one(*pieces[0])
    for cut in pieces[1:]:
        level = level * one(*cut)
    return level


def deal_out(rng, own, number, rows, amount, top, most, slope):
    ranking = jax.random.permutation(rng, amount)
    packed, ordinary = shares(amount, rows * top, most, slope, True), shares(amount, rows * top, most, slope, False)
    places = jnp.arange(amount)

    def named(tallies, rotation):
        used = int((tallies > 0).sum())
        fixed = max(1, used // 4)
        shifted = fixed + (places - fixed + rotation * (used - fixed)) % max(1, amount - fixed)
        return jnp.zeros((amount,), jnp.int32).at[ranking[jnp.where(places < fixed, places, shifted)]].set(jnp.asarray(tallies, jnp.int32))

    tallies = jnp.where(number % 4 == 0, named(packed, number // 4), named(ordinary, number - number // 4 - 1))
    mixed = jax.random.permutation(jax.random.fold_in(own, 3), amount)
    source_of, taker = mixed[0:amount // 2 * 2:2], mixed[1:amount // 2 * 2:2]
    room = jnp.minimum(tallies[source_of] - 1, most - tallies[taker]) // 2
    room = jnp.where((source_of == ranking[0]) | (taker == ranking[0]) | (tallies[taker] == 0), 0, jnp.maximum(room, 0))
    shifted = jax.random.randint(jax.random.fold_in(own, 4), (amount // 2,), 0, 1 << 20) % (room + 1)
    tallies = tallies.at[source_of].add(-shifted).at[taker].add(shifted)
    members = jnp.searchsorted(jnp.cumsum(tallies), jnp.arange(rows * top), side="right").astype(jnp.int32)
    table = members.reshape(top, rows).T
    table = table[jax.random.permutation(jax.random.fold_in(own, 1), rows)]
    rotation = jax.random.randint(jax.random.fold_in(own, 2), (rows, 1), 0, top)
    return jnp.take_along_axis(table, (jnp.arange(top)[None, :] + rotation) % top, axis=1)


def shares(count, total, most, lean, full):
    weights = [(1 << 20) // math.isqrt(grade ** lean) + 1 for grade in range(1, count + 1)]
    largest = most if full else min(most, max(-(-total // count), total * weights[0] // sum(weights)))
    least = 1 if total - largest >= count - 1 else 0
    given, surplus = [largest] + [least] * (count - 1), total - largest - least * (count - 1)
    while surplus > 0:
        free = [i for i in range(1, count) if given[i] < largest] or [i for i in range(1, count) if given[i] < most]
        pool, remaining = sum([weights[i] for i in free]), surplus
        for i in free:
            more = min(most - given[i], max(1, remaining * weights[i] // pool), surplus)
            given[i] = given[i] + more
            surplus = surplus - more
    return np.array(given)


def noise(rng, dims, deviation, reach, pieces=(), kind=jnp.bfloat16):
    entries = jax.random.normal(rng, dims, jnp.float32) * deviation
    if len(pieces) > 0:
        entries = steps_of(rng, dims, pieces, -0.22, 0.18) * entries
    return jnp.clip(entries, min=-reach, max=reach).astype(kind)


def setup_inputs(seed: int = 0) -> dict:
    seeds = jax.random.split(jax.random.key(seed), 13)
    queries = noise(seeds[0], (TOKEN_TOTAL, D), 0.15, 2.0, ((0, 8), (1, 4)))
    keys = noise(seeds[1], (TOKEN_TOTAL, D), 0.15, 2.0, ((0, 8), (1, 4)))
    values = noise(seeds[2], (TOKEN_TOTAL, D), 1.0, 6.0, ((0, 8), (1, 4)))
    log_decay = draw_log_decay(jax.random.fold_in(seeds[12], 71), 0)
    residual = noise(seeds[4], (TOKEN_TOTAL, D), 1.0, 6.0, ((0, 32),))
    attn_gain = jnp.clip(1.0 + 0.15 * jax.random.normal(seeds[5], (D,), jnp.float32), 0.25, 1.75)
    moe_gain = jnp.clip(1.0 + 0.15 * jax.random.normal(seeds[6], (D,), jnp.float32), 0.25, 1.75)
    expert_ids_keys = jax.random.split(jax.random.fold_in(seeds[7], 1), TOKEN_TOTAL // TOK_DEV)
    expert_ids_turns = jax.random.permutation(jax.random.fold_in(seeds[7], 3), TOKEN_TOTAL // TOK_DEV)
    expert_ids = jax.vmap(lambda own, number: deal_out(jax.random.fold_in(seeds[7], 2), own, number, TOK_DEV, EXPERTS, 2, CAP, 2))(expert_ids_keys, expert_ids_turns).reshape((TOKEN_TOTAL, 2))
    gate_weights = jnp.clip(0.2 + 0.8 * jax.random.uniform(seeds[8], (TOKEN_TOTAL, 2), jnp.float32) ** steps_of(seeds[8], (TOKEN_TOTAL, 2), ((0, 32),), -0.2, 0.2), 0.2, 1.0)
    w_gate = noise(seeds[9], (EXPERTS, FF, D), D ** -0.5, 0.09375, ((0, 4), (1, 8)))
    w_up = noise(seeds[10], (EXPERTS, FF, D), D ** -0.5, 0.09375, ((0, 4), (1, 8)))
    w_down = noise(seeds[11], (EXPERTS, FF, D), FF ** -0.5, 0.0625, ((0, 4), (1, 8)))
    return {"queries": queries, "keys": keys, "values": values, "log_decay": log_decay, "residual": residual, "attn_gain": attn_gain, "moe_gain": moe_gain, "expert_ids": expert_ids, "gate_weights": gate_weights, "w_gate": w_gate, "w_up": w_up, "w_down": w_down}


def attend_block(state, inputs):
    q_blk, k_blk, v_blk, decay_blk = inputs
    rows = q_blk.shape[0]
    q_heads = q_blk.reshape(rows, HEAD_TOTAL, HD).astype(jnp.float32)
    k_heads = k_blk.reshape(rows, HEAD_TOTAL, HD).astype(jnp.float32)
    v_heads = v_blk.reshape(rows, HEAD_TOTAL, HD).astype(jnp.float32)
    log_cum = jnp.cumsum(decay_blk, axis=0)
    block_total = log_cum[-1]
    scores = jnp.einsum('thd,shd->hts', q_heads, k_heads)
    gap_logs = log_cum.T[:, :, None] - log_cum.T[:, None, :]
    causal_mask = (lax.broadcasted_iota(jnp.int32, (rows, rows), 0) >= lax.broadcasted_iota(jnp.int32, (rows, rows), 1))[None, :, :]
    weights = jnp.where(causal_mask, scores * jnp.exp(jnp.where(causal_mask, gap_logs, 0.0)), 0.0).astype(jnp.bfloat16)
    intra = jnp.einsum('hts,she->the', weights.astype(jnp.float32), v_heads)
    inter = jnp.exp(log_cum)[:, :, None] * jnp.einsum('thd,hde->the', q_heads, state, precision=lax.Precision.HIGHEST)
    attn = intra + inter
    keys_weighted = (k_heads * jnp.exp(block_total[None, :] - log_cum)[:, :, None]).astype(jnp.bfloat16)
    block_state = jnp.einsum('thd,the->hde', keys_weighted.astype(jnp.float32), v_heads)
    new_state = jnp.exp(block_total)[:, None, None] * state + block_state
    normed = (attn * lax.rsqrt(lax.optimization_barrier(jnp.mean(attn * attn, axis=-1, keepdims=True)) + 1e-06)).astype(jnp.bfloat16)
    return (new_state, normed.reshape(rows, HEAD_TOTAL * HD))

def route_targets(ids_block):
    flat_ids = ids_block.reshape(-1).astype(jnp.int32)
    onehot = (flat_ids[:, None] == jnp.arange(EXPERTS, dtype=jnp.int32)[None, :]).astype(jnp.int32)
    before = jnp.cumsum(onehot, axis=0) - onehot
    slot_index = lax.optimization_barrier(jnp.sum(before * onehot, axis=1)).astype(jnp.int32)
    return (flat_ids * CAP + slot_index).astype(jnp.int32)

def reference(queries, keys, values, log_decay, residual, attn_gain, moe_gain, expert_ids, gate_weights, w_gate, w_up, w_down):
    width = HEAD_TOTAL * HD
    blocks = TOKEN_TOTAL // BLOCK
    q_all = queries.reshape(blocks, BLOCK, width)
    k_all = keys.reshape(blocks, BLOCK, width)
    v_all = values.reshape(blocks, BLOCK, width)
    d_all = log_decay.reshape(blocks, BLOCK, HEAD_TOTAL)
    start_state = jnp.zeros((HEAD_TOTAL, HD, HD), jnp.float32)
    unused, normed = lax.scan(attend_block, start_state, (q_all, k_all, v_all, d_all))
    normed = normed.reshape(TOKEN_TOTAL, width)
    hidden = (residual.astype(jnp.float32) + normed.astype(jnp.float32) * attn_gain).astype(jnp.bfloat16)
    hid32 = hidden.astype(jnp.float32)
    moe_in = (hid32 * lax.rsqrt(lax.optimization_barrier(jnp.mean(hid32 * hid32, axis=-1, keepdims=True)) + 1e-06) * moe_gain).astype(jnp.bfloat16)
    groups = TOKEN_TOTAL // TOK_DEV
    moe_groups = moe_in.reshape(groups, TOK_DEV, width)
    ids_groups = expert_ids.reshape(groups, TOK_DEV * 2)
    targets = jax.vmap(route_targets)(ids_groups)

    def fill(moe_blk, target):
        doubled = jnp.repeat(moe_blk, 2, axis=0)
        return jnp.zeros((EXPERTS * CAP, width), jnp.bfloat16).at[target].set(doubled)
    buffers = jax.vmap(fill)(moe_groups, targets).reshape(groups, EXPERTS, CAP, width)
    slice_len = FF // N_SEQ

    def one_expert(index):
        rows_in = lax.dynamic_index_in_dim(buffers, index, 1, keepdims=False).reshape(groups * CAP, width).astype(jnp.float32)
        gate_mat = lax.dynamic_index_in_dim(w_gate, index, 0, keepdims=False).astype(jnp.float32)
        up_mat = lax.dynamic_index_in_dim(w_up, index, 0, keepdims=False).astype(jnp.float32)
        down_mat = lax.dynamic_index_in_dim(w_down, index, 0, keepdims=False).astype(jnp.float32)
        gate_part = jnp.dot(rows_in, gate_mat.T, preferred_element_type=jnp.float32, precision=lax.Precision.HIGHEST)
        up_part = jnp.dot(rows_in, up_mat.T, preferred_element_type=jnp.float32, precision=lax.Precision.HIGHEST)
        active = (jax.nn.silu(gate_part) * up_part).astype(jnp.bfloat16)
        active = lax.optimization_barrier(active).astype(jnp.float32)
        act_slices = active.reshape(groups * CAP, N_SEQ, slice_len).transpose(1, 0, 2)
        down_slices = down_mat.reshape(N_SEQ, slice_len, width)

        def add_slice(total, pair):
            part = jnp.dot(pair[0], pair[1], preferred_element_type=jnp.float32, precision=lax.Precision.HIGHEST).astype(jnp.bfloat16)
            return (total + part.astype(jnp.float32), None)
        total, unused_parts = lax.scan(add_slice, jnp.zeros((groups * CAP, width), jnp.float32), (act_slices, down_slices))
        return total.astype(jnp.bfloat16).reshape(groups, CAP, width)
    expert_out = lax.map(one_expert, jnp.arange(EXPERTS, dtype=jnp.int32))
    expert_out = expert_out.transpose(1, 0, 2, 3).reshape(groups, EXPERTS * CAP, width)

    def pick_rows(table, target):
        return table[target]
    picked = jax.vmap(pick_rows)(expert_out, targets).reshape(groups, TOK_DEV, 2, width)
    gates = gate_weights.reshape(groups, TOK_DEV, 2)
    mixed = hid32.reshape(groups, TOK_DEV, width) + lax.optimization_barrier(jnp.sum(gates[:, :, :, None] * picked.astype(jnp.float32), axis=2))
    return mixed.astype(jnp.bfloat16).reshape(TOKEN_TOTAL, width)
```

```python
import functools

import jax
import jax.numpy as jnp
from jax import lax
from jax.experimental import pallas as pl
from jax.experimental.pallas import tpu as pltpu
from jax.sharding import PartitionSpec as P

MESH = pl.DeviceIdType.MESH


class Place:
    def __init__(self, n_seq, n_exp):
        s, e = lax.axis_index("seq"), lax.axis_index("exp")
        self.fold, self.n_exp = n_exp // 4, n_exp
        self.length = (n_seq // 2) * self.fold
        self.p = (s // 2) * self.fold + e // 4
        self.x, self.y, self.c = s % 2, (e // 2) % 2, e % 2

    def ids(self, p, x, y, c):
        return (p // self.fold) * 2 + x, (p % self.fold) * 4 + y * 2 + c

    def block(self, p, x, y, c):
        s, e = self.ids(p, x, y, c)
        return s * self.n_exp + e

    def dev(self, dp=0, dx=0, dy=0, dc=0):
        x = 1 - self.x if dx else self.x
        y = 1 - self.y if dy else self.y
        c = 1 - self.c if dc else self.c
        return self.ids(self.p + dp, x, y, c)

    def greet(self):
        barrier = pltpu.get_barrier_semaphore()
        for d in (dict(dx=1), dict(dy=1), dict(dc=1)):
            pl.semaphore_signal(barrier, inc=1, device_id=self.dev(**d), device_id_type=MESH)

        @pl.when(self.p > 0)
        def _():
            pl.semaphore_signal(barrier, inc=1, device_id=self.dev(dp=-1), device_id_type=MESH)

        @pl.when(self.p < self.length - 1)
        def _():
            pl.semaphore_signal(barrier, inc=1, device_id=self.dev(dp=1), device_id_type=MESH)

        ends = (self.p > 0).astype(jnp.int32) + (self.p < self.length - 1).astype(jnp.int32)
        pl.semaphore_wait(barrier, 3 + ends)

    def at(self, stage, sign, k):
        if sign == 0:
            stage(0, 0, 0)
        elif sign < 0:
            pl.when(self.p >= k)(lambda: stage(2 * k - 1, -k, -1))
        else:
            pl.when(self.p + k < self.length)(lambda: stage(2 * k, k, 1))

    def far_first(self, stage):
        def one(i, carry):
            for sign in (1, -1):
                self.at(stage, sign, self.length - 1 - i)
            return carry

        if self.length <= 8:
            for i in range(self.length - 1):
                one(i, 0)
        else:
            lax.fori_loop(0, self.length - 1, one, 0)
        self.at(stage, 0, 0)

    def near_first(self, *stages):
        depth = len(stages)

        def ring(stage, k):
            if isinstance(k, int) and k == 0:
                self.at(stage, 0, 0)
            else:
                for sign in (-1, 1):
                    self.at(stage, sign, k)

        def step(k):
            for j, stage in enumerate(stages):
                if 0 <= k - j < self.length:
                    ring(stage, k - j)

        total = self.length + depth - 1
        if self.length <= 8:
            for k in range(total):
                step(k)
            return
        for k in range(depth):
            step(k)

        def one(k, carry):
            for j, stage in enumerate(stages):
                ring(stage, k - j)
            return carry

        lax.fori_loop(depth, self.length, one, 0)
        for k in range(self.length, total):
            step(k)


def gather_kernel(n_seq, n_exp, x_ref, g_ref, out_ref, gout_ref, send, recv, loc):
    me = Place(n_seq, n_exp)
    rows, width = x_ref.shape
    grow = g_ref.shape[0]
    me.greet()

    def place(ref, off, dx, dy, dc=0):
        x = 1 - me.x if dx else me.x
        y = 1 - me.y if dy else me.y
        c = 1 - me.c if dc else me.c
        b = me.block(me.p + off, x, y, c)
        n = rows if ref is out_ref else grow
        return ref.at[pl.ds(pl.multiple_of(b * n, n), n)]

    def copies(kind, slot, off, dx, dy, to, own=False, half=None, dc=0):
        dst_x, dst_g = place(out_ref, off, dx, dy, dc), place(gout_ref, off, dx, dy, dc)
        src_x, src_g = (x_ref, g_ref) if own else (dst_x, dst_g)
        if half is not None:
            cols = pl.ds(half * (width // 2), width // 2)
            src_x, dst_x = src_x.at[:, cols], dst_x.at[:, cols]
        out = [
            pltpu.make_async_remote_copy(
                src_x, dst_x, send.at[kind, slot, 0], recv.at[kind, slot, 0], to, MESH
            )
        ]
        if half != 1:
            out.append(
                pltpu.make_async_remote_copy(
                    src_g, dst_g, send.at[kind, slot, 1], recv.at[kind, slot, 1], to, MESH
                )
            )
        return out

    def start(*a, **k):
        for cp in copies(*a, **k):
            cp.start()

    def wait_recv(*a, **k):
        for cp in copies(*a, **k):
            cp.wait_recv()

    def wait_send(*a, **k):
        for cp in copies(*a, **k):
            cp.wait_send()

    left, right = dict(dp=-1), dict(dp=1)
    X, Y, C = me.dev(dx=1), me.dev(dy=1), me.dev(dc=1)

    def line_sends(off, sign, do):
        own = sign == 0
        if sign <= 0:
            pl.when(me.p + 1 < me.length)(
                lambda: do(0, 2 * (-off + 1) - 1, off, 0, 0, me.dev(**right), own=own)
            )
        if sign >= 0:
            pl.when(me.p > 0)(lambda: do(0, 2 * (off + 1), off, 0, 0, me.dev(**left), own=own))

    def stage_line(slot, off, sign, do):
        own = sign == 0
        line_sends(off, sign, do)
        do(1, slot, off, 0, 0, X, own=own)
        do(2, slot, off, 0, 0, Y, own=own)
        do(5, slot, off, 0, 0, C, own=own)

    def stage_xy_1(slot, off, do):
        do(3, slot, off, 1, 0, Y, half=0)
        do(6, slot, off, 1, 0, C)

    def stage_xy_2(slot, off, do):
        do(4, slot, off, 0, 1, X, half=1)
        do(7, slot, off, 0, 1, C)

    def stage_diag(slot, off, do):
        do(8, slot, off, 1, 1, C)

    local = [
        pltpu.make_async_copy(x_ref, place(out_ref, 0, 0, 0), loc.at[0]),
        pltpu.make_async_copy(g_ref, place(gout_ref, 0, 0, 0), loc.at[1]),
    ]
    for cp in local:
        cp.start()

    def s1(slot, off, sign):
        if sign:
            wait_recv(0, slot, off, 0, 0, X)
        stage_line(slot, off, sign, start)

    def s2(slot, off, sign):
        wait_recv(1, slot, off, 1, 0, X)
        stage_xy_1(slot, off, start)
        wait_recv(2, slot, off, 0, 1, X)
        stage_xy_2(slot, off, start)

    def s3(slot, off, sign):
        wait_recv(3, slot, off, 1, 1, X, half=0)
        wait_recv(4, slot, off, 1, 1, X, half=1)
        stage_diag(slot, off, start)

    me.near_first(s1, s2, s3)

    def s4(slot, off, sign):
        stage_line(slot, off, sign, wait_send)
        stage_xy_1(slot, off, wait_send)
        stage_xy_2(slot, off, wait_send)
        stage_diag(slot, off, wait_send)
        wait_recv(5, slot, off, 0, 0, X, dc=1)
        wait_recv(6, slot, off, 1, 0, X, dc=1)
        wait_recv(7, slot, off, 0, 1, X, dc=1)
        wait_recv(8, slot, off, 1, 1, X, dc=1)

    me.near_first(s4)
    for cp in local:
        cp.wait()


def gather_all(x, g, n_seq, n_exp):
    n = n_seq * n_exp
    length = n // 8
    anyspace = pl.BlockSpec(memory_space=pl.ANY)
    return pl.pallas_call(
        functools.partial(gather_kernel, n_seq, n_exp),
        out_shape=(
            jax.ShapeDtypeStruct((n * x.shape[0], x.shape[1]), x.dtype),
            jax.ShapeDtypeStruct((n * g.shape[0], g.shape[1]), g.dtype),
        ),
        in_specs=[anyspace, anyspace],
        out_specs=(anyspace, anyspace),
        scratch_shapes=[
            pltpu.SemaphoreType.DMA((9, 2 * length + 1, 2)),
            pltpu.SemaphoreType.DMA((9, 2 * length + 1, 2)),
            pltpu.SemaphoreType.DMA((2,)),
        ],
        compiler_params=pltpu.CompilerParams(collective_id=1, has_side_effects=True),
    )(x, g)


def scatter_kernel(
    n_seq, n_exp, y_ref, out_ref, acc, sib, xbuf, ybuf, dab, dbb, line, send, recv, loc
):
    me = Place(n_seq, n_exp)
    L = me.length
    rows, width = out_ref.shape
    halfw = width // 2
    me.greet()
    X, Y, C = me.dev(dx=1), me.dev(dy=1), me.dev(dc=1)

    def src(off, grp, dc):
        x = 1 - me.x if grp & 1 else me.x
        y = 1 - me.y if grp & 2 else me.y
        c = 1 - me.c if dc else me.c
        b = me.block(me.p + off, x, y, c)
        return y_ref.at[pl.ds(pl.multiple_of(b * rows, rows), rows)]

    def sib_copy(slot, off, grp):
        return pltpu.make_async_remote_copy(
            src(off, grp, 1), sib.at[grp, slot], send.at[grp, slot], recv.at[grp, slot], C, MESH
        )

    def load(slot, off, grp):
        return pltpu.make_async_copy(src(off, grp, 0), acc.at[grp, slot], loc.at[grp, slot])

    for grp in (3, 1, 2, 0):

        def go(slot, off, sign, grp=grp):
            sib_copy(slot, off, grp).start()
            load(slot, off, grp).start()

        me.far_first(go)

    f32 = jnp.float32

    def pair_sum(slot, off, grp):
        load(slot, off, grp).wait()
        sib_copy(slot, off, grp).wait_recv()
        return acc[grp, slot].astype(f32) + sib[grp, slot].astype(f32)

    def diag_a(slot):
        return pltpu.make_async_remote_copy(
            acc.at[3, slot, :, pl.ds(0, halfw)], dab.at[slot], send.at[4, slot], recv.at[4, slot], Y, MESH
        )

    def diag_b(slot):
        return pltpu.make_async_remote_copy(
            acc.at[3, slot, :, pl.ds(halfw, halfw)], dbb.at[slot], send.at[5, slot], recv.at[5, slot], X, MESH
        )

    def x_copy(slot):
        return pltpu.make_async_remote_copy(
            acc.at[1, slot], xbuf.at[slot], send.at[6, slot], recv.at[6, slot], X, MESH
        )

    def y_copy(slot):
        return pltpu.make_async_remote_copy(
            acc.at[2, slot], ybuf.at[slot], send.at[7, slot], recv.at[7, slot], Y, MESH
        )

    def line_copy(slot, sign):
        return pltpu.make_async_remote_copy(
            acc.at[0, slot],
            line.at[slot],
            send.at[8, slot],
            recv.at[8, slot],
            me.dev(dp=sign),
            MESH,
        )

    def d1(slot, off, sign):
        acc[3, slot] = pair_sum(slot, off, 3).astype(acc.dtype)
        diag_a(slot).start()
        diag_b(slot).start()

    def d2(slot, off, sign):
        sx = pair_sum(slot, off, 1)
        diag_a(slot).wait_recv()
        acc[1, slot, :, pl.ds(0, halfw)] = (sx[:, :halfw] + dab[slot].astype(f32)).astype(acc.dtype)
        acc[1, slot, :, pl.ds(halfw, halfw)] = sx[:, halfw:].astype(acc.dtype)
        x_copy(slot).start()
        sy = pair_sum(slot, off, 2)
        diag_b(slot).wait_recv()
        acc[2, slot, :, pl.ds(0, halfw)] = sy[:, :halfw].astype(acc.dtype)
        acc[2, slot, :, pl.ds(halfw, halfw)] = (sy[:, halfw:] + dbb[slot].astype(f32)).astype(acc.dtype)
        y_copy(slot).start()

    def d3(slot, off, sign):
        total = pair_sum(slot, off, 0)
        x_copy(slot).wait_recv()
        y_copy(slot).wait_recv()
        total = total + xbuf[slot].astype(f32) + ybuf[slot].astype(f32)
        if sign == 0:
            out_ref[...] = total
            if L > 1:

                @pl.when(me.p > 0)
                def _():
                    in_copy(2).wait_recv()
                    out_ref[...] += line[2].astype(f32)

                @pl.when(me.p < L - 1)
                def _():
                    in_copy(1).wait_recv()
                    out_ref[...] += line[1].astype(f32)

            return
        acc[0, slot] = total.astype(acc.dtype)
        far = slot + 2
        behind = me.p > 0 if sign > 0 else me.p < L - 1

        @pl.when(jnp.logical_and(behind, sign * off + 1 < L))
        def _():
            in_copy(far).wait_recv()
            acc[0, slot] = (acc[0, slot].astype(f32) + line[far].astype(f32)).astype(acc.dtype)

        line_copy(slot, sign).start()

    def in_copy(slot):
        return pltpu.make_async_remote_copy(
            acc.at[0, slot], line.at[slot], send.at[8, slot], recv.at[8, slot], X, MESH
        )

    me.far_first(d1)
    me.far_first(d2)
    me.far_first(d3)

    def fin(slot, off, sign):
        for grp in range(4):
            sib_copy(slot, off, grp).wait_send()
        diag_a(slot).wait_send()
        diag_b(slot).wait_send()
        x_copy(slot).wait_send()
        y_copy(slot).wait_send()
        if sign:
            line_copy(slot, sign).wait_send()

    me.far_first(fin)


def scatter_sum(part, n_seq, n_exp):
    n = n_seq * n_exp
    slots = n // 4 - 1 + 2
    rows, width = part.shape[0] // n, part.shape[1]
    bf = jnp.bfloat16
    return pl.pallas_call(
        functools.partial(scatter_kernel, n_seq, n_exp),
        out_shape=jax.ShapeDtypeStruct((rows, width), jnp.float32),
        in_specs=[pl.BlockSpec(memory_space=pl.ANY)],
        out_specs=pl.BlockSpec(memory_space=pltpu.VMEM),
        scratch_shapes=[
            pltpu.VMEM((4, slots, rows, width), bf),
            pltpu.VMEM((4, slots, rows, width), bf),
            pltpu.VMEM((slots, rows, width), bf),
            pltpu.VMEM((slots, rows, width), bf),
            pltpu.VMEM((slots, rows, width // 2), bf),
            pltpu.VMEM((slots, rows, width // 2), bf),
            pltpu.VMEM((slots, rows, width), bf),
            pltpu.SemaphoreType.DMA((9, slots)),
            pltpu.SemaphoreType.DMA((9, slots)),
            pltpu.SemaphoreType.DMA((4, slots)),
        ],
        compiler_params=pltpu.CompilerParams(
            collective_id=2, has_side_effects=True, vmem_limit_bytes=60 * 2**20
        ),
    )(part)


def carried_in(value, axis, join, neutral):
    place = lax.axis_index(axis)
    gathered = jax.tree.map(
        lambda a, kind: lax.all_gather(a.astype(kind), axis), value, (jnp.bfloat16, jnp.bfloat16)
    )
    state = jax.tree.map(lambda a, e: jnp.zeros_like(a) + jnp.asarray(e, a.dtype), value, neutral)

    def one(hop, state):
        return join(
            state,
            jax.tree.map(
                lambda a, own: lax.dynamic_index_in_dim(a, hop, 0, False).astype(own.dtype),
                gathered,
                value,
            ),
        )

    return lax.fori_loop(0, place, one, state)


def combine_states(earlier, later):
    return (earlier[0] + later[0], jnp.exp(later[0])[:, None, None] * earlier[1] + later[1])


def body(
    queries,
    keys,
    values,
    log_decay,
    residual,
    attn_gain,
    moe_gain,
    expert_ids,
    gate_weights,
    w_gate,
    w_up,
    w_down,
):
    rows = queries.shape[0]
    heads = log_decay.shape[1]
    head_dim = queries.shape[1] // heads
    q_heads = queries.reshape(rows, heads, head_dim)
    k_heads = keys.reshape(rows, heads, head_dim)
    v_heads = values.reshape(rows, heads, head_dim)
    log_cum = jnp.cumsum(log_decay, axis=0)
    block_total = log_cum[-1]
    keys_weighted = (k_heads * jnp.exp(block_total[None, :] - log_cum)[:, :, None]).astype(
        jnp.bfloat16
    )
    block_state = jnp.einsum(
        "thd,the->hde", keys_weighted, v_heads, preferred_element_type=jnp.float32
    )
    identity_pair = (
        jnp.zeros((heads,), jnp.float32),
        jnp.zeros((heads, head_dim, head_dim), jnp.float32),
    )
    carried = carried_in((block_total, block_state), "seq", combine_states, identity_pair)[1]
    scores = jnp.einsum("thd,shd->hts", q_heads, k_heads, preferred_element_type=jnp.float32)
    gap_logs = log_cum.T[:, :, None] - log_cum.T[:, None, :]
    causal_mask = (
        lax.broadcasted_iota(jnp.int32, (rows, rows), 0)
        >= lax.broadcasted_iota(jnp.int32, (rows, rows), 1)
    )[None, :, :]
    weights = jnp.where(
        causal_mask, scores * jnp.exp(jnp.where(causal_mask, gap_logs, 0.0)), 0.0
    ).astype(jnp.bfloat16)
    intra = jnp.einsum("hts,she->the", weights, v_heads, preferred_element_type=jnp.float32)
    inter = jnp.exp(log_cum)[:, :, None] * jnp.einsum(
        "thd,hde->the", q_heads.astype(jnp.float32), carried, precision=lax.Precision.HIGHEST
    )
    attn = intra + inter
    normed = (attn * lax.rsqrt(jnp.mean(attn * attn, axis=-1, keepdims=True) + 1e-06)).astype(
        jnp.bfloat16
    )
    normed = normed.reshape(rows, heads * head_dim)
    token_major = lax.all_to_all(normed, "exp", split_axis=0, concat_axis=1, tiled=True)
    hidden = (residual.astype(jnp.float32) + token_major.astype(jnp.float32) * attn_gain).astype(
        jnp.bfloat16
    )
    hid32 = hidden.astype(jnp.float32)
    moe_in = (
        hid32 * lax.rsqrt(jnp.mean(hid32 * hid32, axis=-1, keepdims=True) + 1e-06) * moe_gain
    ).astype(jnp.bfloat16)
    n_seq, n_exp = lax.axis_size("seq"), lax.axis_size("exp")
    tok_rows = residual.shape[0]
    experts = w_gate.shape[0] * n_exp
    gates = jnp.sum(
        jnp.where(
            expert_ids[:, :, None] == jnp.arange(experts, dtype=jnp.int32)[None, None, :],
            gate_weights[:, :, None],
            0.0,
        ),
        axis=1,
    )
    flat = gates.T.reshape(-1)
    pad = -flat.shape[0] % 1024
    g_tile = jnp.pad(flat, (0, pad)).reshape(-1, 128)
    everyone, g_all = gather_all(moe_in, g_tile, n_seq, n_exp)
    g_all = g_all.reshape(n_seq * n_exp, -1)[:, : experts * tok_rows]
    g_all = g_all.reshape(n_seq * n_exp, experts, tok_rows)
    mixed = None
    gate_col = lax.dynamic_slice_in_dim(
        g_all, lax.axis_index("exp") * w_gate.shape[0], w_gate.shape[0], 1
    )
    part = None
    for j in range(w_gate.shape[0]):
        gate_part = jnp.einsum("td,fd->tf", everyone, w_gate[j], preferred_element_type=jnp.float32)
        up_part = jnp.einsum("td,fd->tf", everyone, w_up[j], preferred_element_type=jnp.float32)
        active = (
            jax.nn.silu(gate_part) * up_part * gate_col[:, j, :].reshape(-1, 1)
        ).astype(jnp.bfloat16)
        one = jnp.dot(active, w_down[j], preferred_element_type=jnp.float32)
        part = one if part is None else part + one
    part = part.astype(jnp.bfloat16)
    total_rows, width = part.shape
    pieces = max(1, total_rows // 1024)
    step = width // pieces
    summed = [
        jax.jit(scatter_sum, static_argnums=(1, 2))(part[:, i * step : (i + 1) * step], n_seq, n_exp) for i in range(pieces)
    ]
    summed = summed[0] if pieces == 1 else jnp.concatenate(summed, axis=1)
    return (hid32 + summed).astype(jnp.bfloat16)


def solution(mesh):
    in_specs = (
        P("seq", "exp"),
        P("seq", "exp"),
        P("seq", "exp"),
        P("seq", "exp"),
        P(("seq", "exp"), None),
        P(),
        P(),
        P(("seq", "exp"), None),
        P(("seq", "exp"), None),
        P("exp", "seq", None),
        P("exp", "seq", None),
        P("exp", "seq", None),
    )
    out_specs = P(("seq", "exp"), None)
    return jax.shard_map(body, mesh=mesh, in_specs=in_specs, out_specs=out_specs, check_vma=False)
```

```python
import functools

import jax
import jax.numpy as jnp
from jax import lax
from jax.experimental import pallas as pl
from jax.experimental.pallas import tpu as pltpu
from jax.sharding import PartitionSpec as P

MESH = pl.DeviceIdType.MESH


class Place:
    def __init__(self, n_seq, n_exp):
        s, e = lax.axis_index("seq"), lax.axis_index("exp")
        self.fold, self.n_exp = n_exp // 4, n_exp
        self.length = (n_seq // 2) * self.fold
        self.p = (s // 2) * self.fold + e // 4
        self.x, self.y, self.c = s % 2, (e // 2) % 2, e % 2

    def ids(self, p, x, y, c):
        return (p // self.fold) * 2 + x, (p % self.fold) * 4 + y * 2 + c

    def block(self, p, x, y, c):
        s, e = self.ids(p, x, y, c)
        return s * self.n_exp + e

    def dev(self, dp=0, dx=0, dy=0, dc=0):
        x = 1 - self.x if dx else self.x
        y = 1 - self.y if dy else self.y
        c = 1 - self.c if dc else self.c
        return self.ids(self.p + dp, x, y, c)

    def greet(self):
        barrier = pltpu.get_barrier_semaphore()
        for d in (dict(dx=1), dict(dy=1), dict(dc=1)):
            pl.semaphore_signal(barrier, inc=1, device_id=self.dev(**d), device_id_type=MESH)

        @pl.when(self.p > 0)
        def _():
            pl.semaphore_signal(barrier, inc=1, device_id=self.dev(dp=-1), device_id_type=MESH)

        @pl.when(self.p < self.length - 1)
        def _():
            pl.semaphore_signal(barrier, inc=1, device_id=self.dev(dp=1), device_id_type=MESH)

        ends = (self.p > 0).astype(jnp.int32) + (self.p < self.length - 1).astype(jnp.int32)
        pl.semaphore_wait(barrier, 3 + ends)

    def at(self, stage, sign, k):
        if sign == 0:
            stage(0, 0, 0)
        elif sign < 0:
            pl.when(self.p >= k)(lambda: stage(2 * k - 1, -k, -1))
        else:
            pl.when(self.p + k < self.length)(lambda: stage(2 * k, k, 1))

    def far_first(self, stage):
        def one(i, carry):
            for sign in (1, -1):
                self.at(stage, sign, self.length - 1 - i)
            return carry

        if self.length <= 8:
            for i in range(self.length - 1):
                one(i, 0)
        else:
            lax.fori_loop(0, self.length - 1, one, 0)
        self.at(stage, 0, 0)

    def near_first(self, *stages):
        depth = len(stages)

        def ring(stage, k):
            if isinstance(k, int) and k == 0:
                self.at(stage, 0, 0)
            else:
                for sign in (-1, 1):
                    self.at(stage, sign, k)

        def step(k):
            for j, stage in enumerate(stages):
                if 0 <= k - j < self.length:
                    ring(stage, k - j)

        total = self.length + depth - 1
        if self.length <= 8:
            for k in range(total):
                step(k)
            return
        for k in range(depth):
            step(k)

        def one(k, carry):
            for j, stage in enumerate(stages):
                ring(stage, k - j)
            return carry

        lax.fori_loop(depth, self.length, one, 0)
        for k in range(self.length, total):
            step(k)


def gather_kernel(n_seq, n_exp, x_ref, g_ref, out_ref, gout_ref, send, recv, loc):
    me = Place(n_seq, n_exp)
    rows, width = x_ref.shape
    grow = g_ref.shape[0]
    me.greet()

    def place(ref, off, dx, dy, dc=0):
        x = 1 - me.x if dx else me.x
        y = 1 - me.y if dy else me.y
        c = 1 - me.c if dc else me.c
        b = me.block(me.p + off, x, y, c)
        n = rows if ref is out_ref else grow
        return ref.at[pl.ds(pl.multiple_of(b * n, n), n)]

    def copies(kind, slot, off, dx, dy, to, own=False, half=None, dc=0):
        dst_x, dst_g = place(out_ref, off, dx, dy, dc), place(gout_ref, off, dx, dy, dc)
        src_x, src_g = (x_ref, g_ref) if own else (dst_x, dst_g)
        if half is not None:
            cols = pl.ds(half * (width // 2), width // 2)
            src_x, dst_x = src_x.at[:, cols], dst_x.at[:, cols]
        out = [
            pltpu.make_async_remote_copy(
                src_x, dst_x, send.at[kind, slot, 0], recv.at[kind, slot, 0], to, MESH
            )
        ]
        if half != 1:
            out.append(
                pltpu.make_async_remote_copy(
                    src_g, dst_g, send.at[kind, slot, 1], recv.at[kind, slot, 1], to, MESH
                )
            )
        return out

    def start(*a, **k):
        for cp in copies(*a, **k):
            cp.start()

    def wait_recv(*a, **k):
        for cp in copies(*a, **k):
            cp.wait_recv()

    def wait_send(*a, **k):
        for cp in copies(*a, **k):
            cp.wait_send()

    left, right = dict(dp=-1), dict(dp=1)
    X, Y, C = me.dev(dx=1), me.dev(dy=1), me.dev(dc=1)

    def line_sends(off, sign, do):
        own = sign == 0
        if sign <= 0:
            pl.when(me.p + 1 < me.length)(
                lambda: do(0, 2 * (-off + 1) - 1, off, 0, 0, me.dev(**right), own=own)
            )
        if sign >= 0:
            pl.when(me.p > 0)(lambda: do(0, 2 * (off + 1), off, 0, 0, me.dev(**left), own=own))

    def stage_line(slot, off, sign, do):
        own = sign == 0
        line_sends(off, sign, do)
        do(1, slot, off, 0, 0, X, own=own)
        do(2, slot, off, 0, 0, Y, own=own)
        do(5, slot, off, 0, 0, C, own=own)

    def stage_xy_1(slot, off, do):
        do(3, slot, off, 1, 0, Y, half=0)
        do(6, slot, off, 1, 0, C)

    def stage_xy_2(slot, off, do):
        do(4, slot, off, 0, 1, X, half=1)
        do(7, slot, off, 0, 1, C)

    def stage_diag(slot, off, do):
        do(8, slot, off, 1, 1, C)

    local = [
        pltpu.make_async_copy(x_ref, place(out_ref, 0, 0, 0), loc.at[0]),
        pltpu.make_async_copy(g_ref, place(gout_ref, 0, 0, 0), loc.at[1]),
    ]
    for cp in local:
        cp.start()

    def s1(slot, off, sign):
        if sign:
            wait_recv(0, slot, off, 0, 0, X)
        stage_line(slot, off, sign, start)

    def s2(slot, off, sign):
        wait_recv(1, slot, off, 1, 0, X)
        stage_xy_1(slot, off, start)
        wait_recv(2, slot, off, 0, 1, X)
        stage_xy_2(slot, off, start)

    def s3(slot, off, sign):
        wait_recv(3, slot, off, 1, 1, X, half=0)
        wait_recv(4, slot, off, 1, 1, X, half=1)
        stage_diag(slot, off, start)

    me.near_first(s1, s2, s3)

    def s4(slot, off, sign):
        stage_line(slot, off, sign, wait_send)
        stage_xy_1(slot, off, wait_send)
        stage_xy_2(slot, off, wait_send)
        stage_diag(slot, off, wait_send)
        wait_recv(5, slot, off, 0, 0, X, dc=1)
        wait_recv(6, slot, off, 1, 0, X, dc=1)
        wait_recv(7, slot, off, 0, 1, X, dc=1)
        wait_recv(8, slot, off, 1, 1, X, dc=1)

    me.near_first(s4)
    for cp in local:
        cp.wait()


def gather_all(x, g, n_seq, n_exp):
    n = n_seq * n_exp
    length = n // 8
    anyspace = pl.BlockSpec(memory_space=pl.ANY)
    return pl.pallas_call(
        functools.partial(gather_kernel, n_seq, n_exp),
        out_shape=(
            jax.ShapeDtypeStruct((n * x.shape[0], x.shape[1]), x.dtype),
            jax.ShapeDtypeStruct((n * g.shape[0], g.shape[1]), g.dtype),
        ),
        in_specs=[anyspace, anyspace],
        out_specs=(anyspace, anyspace),
        scratch_shapes=[
            pltpu.SemaphoreType.DMA((9, 2 * length + 1, 2)),
            pltpu.SemaphoreType.DMA((9, 2 * length + 1, 2)),
            pltpu.SemaphoreType.DMA((2,)),
        ],
        compiler_params=pltpu.CompilerParams(collective_id=1, has_side_effects=True),
    )(x, g)


def scatter_kernel(
    n_seq, n_exp, y_ref, out_ref, acc, sib, xbuf, ybuf, dab, dbb, line, send, recv, loc
):
    me = Place(n_seq, n_exp)
    L = me.length
    rows, width = out_ref.shape
    halfw = width // 2
    me.greet()
    X, Y, C = me.dev(dx=1), me.dev(dy=1), me.dev(dc=1)

    def src(off, grp, dc):
        x = 1 - me.x if grp & 1 else me.x
        y = 1 - me.y if grp & 2 else me.y
        c = 1 - me.c if dc else me.c
        b = me.block(me.p + off, x, y, c)
        return y_ref.at[pl.ds(pl.multiple_of(b * rows, rows), rows)]

    def sib_copy(slot, off, grp):
        return pltpu.make_async_remote_copy(
            src(off, grp, 1), sib.at[grp, slot], send.at[grp, slot], recv.at[grp, slot], C, MESH
        )

    def load(slot, off, grp):
        return pltpu.make_async_copy(src(off, grp, 0), acc.at[grp, slot], loc.at[grp, slot])

    for grp in (3, 1, 2, 0):

        def go(slot, off, sign, grp=grp):
            sib_copy(slot, off, grp).start()
            load(slot, off, grp).start()

        me.far_first(go)

    f32 = jnp.float32

    def pair_sum(slot, off, grp):
        load(slot, off, grp).wait()
        sib_copy(slot, off, grp).wait_recv()
        return acc[grp, slot].astype(f32) + sib[grp, slot].astype(f32)

    def diag_a(slot):
        return pltpu.make_async_remote_copy(
            acc.at[3, slot, :, pl.ds(0, halfw)], dab.at[slot], send.at[4, slot], recv.at[4, slot], Y, MESH
        )

    def diag_b(slot):
        return pltpu.make_async_remote_copy(
            acc.at[3, slot, :, pl.ds(halfw, halfw)], dbb.at[slot], send.at[5, slot], recv.at[5, slot], X, MESH
        )

    def x_copy(slot):
        return pltpu.make_async_remote_copy(
            acc.at[1, slot], xbuf.at[slot], send.at[6, slot], recv.at[6, slot], X, MESH
        )

    def y_copy(slot):
        return pltpu.make_async_remote_copy(
            acc.at[2, slot], ybuf.at[slot], send.at[7, slot], recv.at[7, slot], Y, MESH
        )

    def line_copy(slot, sign):
        return pltpu.make_async_remote_copy(
            acc.at[0, slot],
            line.at[slot],
            send.at[8, slot],
            recv.at[8, slot],
            me.dev(dp=sign),
            MESH,
        )

    def d1(slot, off, sign):
        acc[3, slot] = pair_sum(slot, off, 3).astype(acc.dtype)
        diag_a(slot).start()
        diag_b(slot).start()

    def d2(slot, off, sign):
        sx = pair_sum(slot, off, 1)
        diag_a(slot).wait_recv()
        acc[1, slot, :, pl.ds(0, halfw)] = (sx[:, :halfw] + dab[slot].astype(f32)).astype(acc.dtype)
        acc[1, slot, :, pl.ds(halfw, halfw)] = sx[:, halfw:].astype(acc.dtype)
        x_copy(slot).start()
        sy = pair_sum(slot, off, 2)
        diag_b(slot).wait_recv()
        acc[2, slot, :, pl.ds(0, halfw)] = sy[:, :halfw].astype(acc.dtype)
        acc[2, slot, :, pl.ds(halfw, halfw)] = (sy[:, halfw:] + dbb[slot].astype(f32)).astype(acc.dtype)
        y_copy(slot).start()

    def d3(slot, off, sign):
        total = pair_sum(slot, off, 0)
        x_copy(slot).wait_recv()
        y_copy(slot).wait_recv()
        total = total + xbuf[slot].astype(f32) + ybuf[slot].astype(f32)
        if sign == 0:
            out_ref[...] = total
            if L > 1:

                @pl.when(me.p > 0)
                def _():
                    in_copy(2).wait_recv()
                    out_ref[...] += line[2].astype(f32)

                @pl.when(me.p < L - 1)
                def _():
                    in_copy(1).wait_recv()
                    out_ref[...] += line[1].astype(f32)

            return
        acc[0, slot] = total.astype(acc.dtype)
        far = slot + 2
        behind = me.p > 0 if sign > 0 else me.p < L - 1

        @pl.when(jnp.logical_and(behind, sign * off + 1 < L))
        def _():
            in_copy(far).wait_recv()
            acc[0, slot] = (acc[0, slot].astype(f32) + line[far].astype(f32)).astype(acc.dtype)

        line_copy(slot, sign).start()

    def in_copy(slot):
        return pltpu.make_async_remote_copy(
            acc.at[0, slot], line.at[slot], send.at[8, slot], recv.at[8, slot], X, MESH
        )

    me.far_first(d1)
    me.far_first(d2)
    me.far_first(d3)

    def fin(slot, off, sign):
        for grp in range(4):
            sib_copy(slot, off, grp).wait_send()
        diag_a(slot).wait_send()
        diag_b(slot).wait_send()
        x_copy(slot).wait_send()
        y_copy(slot).wait_send()
        if sign:
            line_copy(slot, sign).wait_send()

    me.far_first(fin)


def scatter_sum(part, n_seq, n_exp):
    n = n_seq * n_exp
    slots = n // 4 - 1 + 2
    rows, width = part.shape[0] // n, part.shape[1]
    bf = jnp.bfloat16
    return pl.pallas_call(
        functools.partial(scatter_kernel, n_seq, n_exp),
        out_shape=jax.ShapeDtypeStruct((rows, width), jnp.float32),
        in_specs=[pl.BlockSpec(memory_space=pl.ANY)],
        out_specs=pl.BlockSpec(memory_space=pltpu.VMEM),
        scratch_shapes=[
            pltpu.VMEM((4, slots, rows, width), bf),
            pltpu.VMEM((4, slots, rows, width), bf),
            pltpu.VMEM((slots, rows, width), bf),
            pltpu.VMEM((slots, rows, width), bf),
            pltpu.VMEM((slots, rows, width // 2), bf),
            pltpu.VMEM((slots, rows, width // 2), bf),
            pltpu.VMEM((slots, rows, width), bf),
            pltpu.SemaphoreType.DMA((9, slots)),
            pltpu.SemaphoreType.DMA((9, slots)),
            pltpu.SemaphoreType.DMA((4, slots)),
        ],
        compiler_params=pltpu.CompilerParams(
            collective_id=2, has_side_effects=True, vmem_limit_bytes=60 * 2**20
        ),
    )(part)


def carry_kernel(n_seq, own_ref, own16_ref, tot_ref, out_ref, peer, ptot, cin, cout, send, recv, tsem):
    s, e = lax.axis_index("seq"), lax.axis_index("exp")
    z, odd, deep = s // 2, s % 2, n_seq // 2
    heads = own_ref.shape[0]
    pair = (z * 2 + 1 - odd, e)

    barrier = pltpu.get_barrier_semaphore()
    pl.semaphore_signal(barrier, inc=1, device_id=pair, device_id_type=MESH)

    @pl.when(z > 0)
    def _():
        pl.semaphore_signal(barrier, inc=1, device_id=(s - 2, e), device_id_type=MESH)

    @pl.when(z < deep - 1)
    def _():
        pl.semaphore_signal(barrier, inc=1, device_id=(s + 2, e), device_id_type=MESH)

    ends = (z > 0).astype(jnp.int32) + (z < deep - 1).astype(jnp.int32)
    pl.semaphore_wait(barrier, 1 + ends)

    tot_copy = pltpu.make_async_remote_copy(tot_ref, ptot, tsem.at[0], tsem.at[1], pair, MESH)

    def pair_copy(h):
        return pltpu.make_async_remote_copy(
            own16_ref.at[h], peer.at[h], send.at[0, h], recv.at[0, h], pair, MESH
        )

    def line_copy(h):
        return pltpu.make_async_remote_copy(
            cout.at[h], cin.at[h], send.at[1, h], recv.at[1, h], (s + 2, e), MESH
        )

    tot_copy.start()
    for h in range(heads):
        pair_copy(h).start()

    @pl.when(z == 0)
    def _():
        cin[...] = jnp.zeros_like(cin)

    tot_copy.wait_recv()
    mine, other = tot_ref[...], ptot[...]
    both = jnp.exp(mine + other)
    is_odd = jnp.full(mine.shape, odd, jnp.int32) == 1
    one = jnp.ones_like(mine)
    own_by = jnp.where(is_odd, one, jnp.exp(other))
    peer_by = jnp.where(is_odd, jnp.exp(mine), one)
    carry_by = jnp.where(is_odd, jnp.exp(other), one)
    peer_in = jnp.where(is_odd, one, jnp.zeros_like(mine))
    for h in range(heads):
        pair_copy(h).wait_recv()

        @pl.when(z > 0)
        def _():
            line_copy(h).wait_recv()

        near = peer[h].astype(jnp.float32)
        come = cin[h].astype(jnp.float32)

        @pl.when(z < deep - 1)
        def _():
            cout[h] = (
                both[h : h + 1] * come + own_by[h : h + 1] * own_ref[h] + peer_by[h : h + 1] * near
            ).astype(cout.dtype)
            line_copy(h).start()

        out_ref[h] = carry_by[h : h + 1] * come + peer_in[h : h + 1] * near

    tot_copy.wait_send()
    for h in range(heads):
        pair_copy(h).wait_send()

        @pl.when(z < deep - 1)
        def _():
            line_copy(h).wait_send()


def carried_in(block_total, block_state, n_seq):
    heads, dim, _ = block_state.shape
    bf = jnp.bfloat16
    tile = jnp.pad(block_total, (0, -heads % 8))
    tile = jnp.broadcast_to(tile[:, None], (tile.shape[0], dim))
    vmem = pl.BlockSpec(memory_space=pltpu.VMEM)
    return pl.pallas_call(
        functools.partial(carry_kernel, n_seq),
        out_shape=jax.ShapeDtypeStruct(block_state.shape, jnp.float32),
        in_specs=[vmem] * 3,
        out_specs=vmem,
        scratch_shapes=[
            pltpu.VMEM(block_state.shape, bf),
            pltpu.VMEM(tile.shape, jnp.float32),
            pltpu.VMEM(block_state.shape, bf),
            pltpu.VMEM(block_state.shape, bf),
            pltpu.SemaphoreType.DMA((2, heads)),
            pltpu.SemaphoreType.DMA((2, heads)),
            pltpu.SemaphoreType.DMA((2,)),
        ],
        compiler_params=pltpu.CompilerParams(collective_id=3, has_side_effects=True),
    )(block_state, block_state.astype(bf), tile)


def body(
    queries,
    keys,
    values,
    log_decay,
    residual,
    attn_gain,
    moe_gain,
    expert_ids,
    gate_weights,
    w_gate,
    w_up,
    w_down,
):
    rows = queries.shape[0]
    heads = log_decay.shape[1]
    head_dim = queries.shape[1] // heads
    q_heads = queries.reshape(rows, heads, head_dim)
    k_heads = keys.reshape(rows, heads, head_dim)
    v_heads = values.reshape(rows, heads, head_dim)
    log_cum = jnp.cumsum(log_decay, axis=0)
    block_total = log_cum[-1]
    keys_weighted = (k_heads * jnp.exp(block_total[None, :] - log_cum)[:, :, None]).astype(
        jnp.bfloat16
    )
    block_state = jnp.einsum(
        "thd,the->hde", keys_weighted, v_heads, preferred_element_type=jnp.float32
    )
    carried = carried_in(block_total, block_state, lax.axis_size("seq"))
    scores = jnp.einsum("thd,shd->hts", q_heads, k_heads, preferred_element_type=jnp.float32)
    gap_logs = log_cum.T[:, :, None] - log_cum.T[:, None, :]
    causal_mask = (
        lax.broadcasted_iota(jnp.int32, (rows, rows), 0)
        >= lax.broadcasted_iota(jnp.int32, (rows, rows), 1)
    )[None, :, :]
    weights = jnp.where(
        causal_mask, scores * jnp.exp(jnp.where(causal_mask, gap_logs, 0.0)), 0.0
    ).astype(jnp.bfloat16)
    intra = jnp.einsum("hts,she->the", weights, v_heads, preferred_element_type=jnp.float32)
    inter = jnp.exp(log_cum)[:, :, None] * jnp.einsum(
        "thd,hde->the", q_heads.astype(jnp.float32), carried, precision=lax.Precision.HIGHEST
    )
    attn = intra + inter
    normed = (attn * lax.rsqrt(jnp.mean(attn * attn, axis=-1, keepdims=True) + 1e-06)).astype(
        jnp.bfloat16
    )
    normed = normed.reshape(rows, heads * head_dim)
    token_major = lax.all_to_all(normed, "exp", split_axis=0, concat_axis=1, tiled=True)
    hidden = (residual.astype(jnp.float32) + token_major.astype(jnp.float32) * attn_gain).astype(
        jnp.bfloat16
    )
    hid32 = hidden.astype(jnp.float32)
    moe_in = (
        hid32 * lax.rsqrt(jnp.mean(hid32 * hid32, axis=-1, keepdims=True) + 1e-06) * moe_gain
    ).astype(jnp.bfloat16)
    n_seq, n_exp = lax.axis_size("seq"), lax.axis_size("exp")
    tok_rows = residual.shape[0]
    experts = w_gate.shape[0] * n_exp
    gates = jnp.sum(
        jnp.where(
            expert_ids[:, :, None] == jnp.arange(experts, dtype=jnp.int32)[None, None, :],
            gate_weights[:, :, None],
            0.0,
        ),
        axis=1,
    )
    flat = gates.T.reshape(-1)
    pad = -flat.shape[0] % 1024
    g_tile = jnp.pad(flat, (0, pad)).reshape(-1, 128)
    everyone, g_all = gather_all(moe_in, g_tile, n_seq, n_exp)
    g_all = g_all.reshape(n_seq * n_exp, -1)[:, : experts * tok_rows]
    g_all = g_all.reshape(n_seq * n_exp, experts, tok_rows)
    mixed = None
    gate_col = lax.dynamic_slice_in_dim(
        g_all, lax.axis_index("exp") * w_gate.shape[0], w_gate.shape[0], 1
    )
    part = None
    for j in range(w_gate.shape[0]):
        gate_part = jnp.einsum("td,fd->tf", everyone, w_gate[j], preferred_element_type=jnp.float32)
        up_part = jnp.einsum("td,fd->tf", everyone, w_up[j], preferred_element_type=jnp.float32)
        active = (
            jax.nn.silu(gate_part) * up_part * gate_col[:, j, :].reshape(-1, 1)
        ).astype(jnp.bfloat16)
        one = jnp.dot(active, w_down[j], preferred_element_type=jnp.float32)
        part = one if part is None else part + one
    part = part.astype(jnp.bfloat16)
    total_rows, width = part.shape
    pieces = max(1, total_rows // 1024)
    step = width // pieces
    summed = [
        jax.jit(scatter_sum, static_argnums=(1, 2))(part[:, i * step : (i + 1) * step], n_seq, n_exp) for i in range(pieces)
    ]
    summed = summed[0] if pieces == 1 else jnp.concatenate(summed, axis=1)
    return (hid32 + summed).astype(jnp.bfloat16)


def solution(mesh):
    in_specs = (
        P("seq", "exp"),
        P("seq", "exp"),
        P("seq", "exp"),
        P("seq", "exp"),
        P(("seq", "exp"), None),
        P(),
        P(),
        P(("seq", "exp"), None),
        P(("seq", "exp"), None),
        P("exp", "seq", None),
        P("exp", "seq", None),
        P("exp", "seq", None),
    )
    out_specs = P(("seq", "exp"), None)
    return jax.shard_map(body, mesh=mesh, in_specs=in_specs, out_specs=out_specs, check_vma=False)
```
